32 devices in a mesh: groups: 1, ctx: 2 (over x), fsdp: 16 (over z, y, core).
Axes of the slice: x: 2, y: 2, z: 4, core: 2. Of those that a mesh axis runs over, the one named last changes fastest.
Arguments:
- tokens: bfloat16 [16, 256, 3072], P(('groups', 'fsdp'), 'ctx'), may hold values from -600 to 600
- trace_index: int32 [16, 256], P(('groups', 'fsdp'), 'ctx'), may hold values from 0 to 1, never falling along the last dimension, each value on 1 to 192 neighbouring positions
- input_norm_scale: bfloat16 [3072], replicated, may hold values from 0.099609375 to 1.8984375
- query_weight: bfloat16 [3072, 2048], P('fsdp'), may hold values from -0.109375 to 0.109375
- key_weight: bfloat16 [3072, 1024], P('fsdp'), may hold values from -0.109375 to 0.109375
- value_weight: bfloat16 [3072, 1024], P('fsdp'), may hold values from -0.109375 to 0.109375
- query_down_weight: bfloat16 [3072, 16], replicated, may hold values from -0.109375 to 0.109375
- query_up_weight: bfloat16 [16, 2048], replicated, may hold values from -1.5 to 1.5
- value_down_weight: bfloat16 [3072, 16], replicated, may hold values from -0.109375 to 0.109375
- value_up_weight: bfloat16 [16, 1024], replicated, may hold values from -1.5 to 1.5
- output_gradient: bfloat16 [16, 256, 2048], P(('groups', 'fsdp'), 'ctx'), may hold values from -24 to 24
Outputs:
- grad_a_query: float32 [3072, 16], P('groups')
- grad_b_query: float32 [16, 2048], P('groups')
- grad_a_value: float32 [3072, 16], P('groups')
- grad_b_value: float32 [16, 1024], P('groups')
The draws below stay inside these ranges and needn't reach their ends.
Inputs may be any that keep to these rules, and one draw needn't show every extreme that they name: `trace_index`: ids never fall along a sequence; one trace holds at most 192 positions.
All inputs are finite; a program needn't handle non-finite values.
Results may differ from the reference program's by a relative error of at most 0.013.
Values may be sent and summed in bfloat16 or wider, within the bound.
A program may use at most 128 MiB of HBM per device.

```python
import math
import jax
import jax.numpy as jnp
import numpy as np
from jax import lax

MODEL_FEATURES = 3072
QUERY_HEADS = 16
KEY_VALUE_HEADS = 8
HEAD_SIZE = 128
ADAPTER_RANK = 16
TOK_DEV = 128
WINDOW = 256
SEQ = 256
TRACES = 2
TRACE = 192
NSEQ = 16
TOKEN_COUNT = 4096


def draw_tokens(key, part):
    first, second, third = jax.random.split(key, 3)
    base = jnp.clip(jax.random.normal(first, (NSEQ, SEQ, MODEL_FEATURES), jnp.float32), -6.0, 6.0)
    row_scale = jnp.exp(jax.random.uniform(second, (NSEQ, SEQ, 1), jnp.float32, 0.0, math.log(10.0)))
    col_scale = jnp.exp(jax.random.uniform(third, (MODEL_FEATURES,), jnp.float32, 0.0, math.log(10.0)))
    return (base * row_scale * col_scale).astype(jnp.bfloat16)


def shard_levels(stream_key, shape, shards, least, high):
    level, own = 1.0, jax.random.fold_in(stream_key, 6)
    for position, parts in shards:
        steps = jnp.exp(jax.random.uniform(jax.random.fold_in(own, position), (parts,), jnp.float32, least / len(shards), high / len(shards)))
        level = level * jnp.repeat(steps, shape[position] // parts).reshape([-1 if axis == position else 1 for axis in range(len(shape))])
    return level


def length_profile(amount, total, limit, lean):
    weights = [(1 << 20) // math.isqrt(rank ** lean) + 1 for rank in range(2, amount + 1)]
    rest, counts = total - limit - (amount - 1), [1] * (amount - 1)
    while rest > 0:
        free = [i for i in range(amount - 1) if counts[i] < limit]
        whole, remaining = sum([weights[i] for i in free]), rest
        for i in free:
            extra = min(limit - counts[i], max(1, remaining * weights[i] // whole), rest)
            counts[i] = counts[i] + extra
            rest = rest - extra
    return np.array([limit] + counts)


def ragged_sizes(own_key, count, total, most, slope):
    if count == 2:
        one = jax.random.randint(own_key, (), max(1, total - most), min(most, total - 1) + 1)
        return jnp.stack([one, total - one])
    lengths = jnp.asarray(length_profile(count, total, most, slope), jnp.int32)
    pairs = (count - 1) // 2
    donor, sink = lengths[1:1 + 2 * pairs:2], lengths[2:2 + 2 * pairs:2]
    margin = jnp.minimum(donor - 1, most - sink)
    moved = jax.random.randint(jax.random.fold_in(own_key, 1), (pairs,), 0, 1 << 20) % (margin + 1)
    lengths = lengths.at[1:1 + 2 * pairs:2].set(donor - moved).at[2:2 + 2 * pairs:2].set(sink + moved)
    return lengths[jax.random.permutation(jax.random.fold_in(own_key, 2), count)]


def bell_draw(key, extent, deviation, reach, shards=(), kind=jnp.bfloat16):
    drawn = jax.random.normal(key, extent, jnp.float32) * deviation
    if len(shards) > 0:
        drawn = shard_levels(key, extent, shards, -0.22, 0.18) * drawn
    return jnp.clip(drawn, min=-reach, max=reach).astype(kind)


def setup_inputs(seed: int = 0, part: int = 0) -> dict:
    key_of = jax.random.split(jax.random.key(seed), 12)
    own_keys = jax.random.split(jax.random.fold_in(key_of[11], part), 12)
    return {
        "tokens": draw_tokens(jax.random.fold_in(jax.random.fold_in(key_of[11], part), 71), part),
        "trace_index": jax.vmap(lambda own: jnp.searchsorted(jnp.cumsum(ragged_sizes(own, TRACES, SEQ, TRACE, 0)), jnp.arange(SEQ), side="right"))(jax.random.split(own_keys[1], NSEQ)).reshape((NSEQ, SEQ)).astype(jnp.int32),
        "input_norm_scale": jnp.clip(1.0 + 0.18 * jax.random.normal(key_of[2], (MODEL_FEATURES,), jnp.float32), 0.099609375, 1.8984375).astype(jnp.bfloat16),
        "query_weight": bell_draw(key_of[3], (MODEL_FEATURES, QUERY_HEADS * HEAD_SIZE), MODEL_FEATURES ** -0.5, 0.109375, ((0, 16),)),
        "key_weight": bell_draw(key_of[4], (MODEL_FEATURES, KEY_VALUE_HEADS * HEAD_SIZE), MODEL_FEATURES ** -0.5, 0.109375, ((0, 16),)),
        "value_weight": bell_draw(key_of[5], (MODEL_FEATURES, KEY_VALUE_HEADS * HEAD_SIZE), MODEL_FEATURES ** -0.5, 0.109375, ((0, 16),)),
        "query_down_weight": bell_draw(key_of[6], (MODEL_FEATURES, ADAPTER_RANK), MODEL_FEATURES ** -0.5, 0.109375),
        "query_up_weight": bell_draw(key_of[7], (ADAPTER_RANK, QUERY_HEADS * HEAD_SIZE), ADAPTER_RANK ** -0.5, 1.5),
        "value_down_weight": bell_draw(key_of[8], (MODEL_FEATURES, ADAPTER_RANK), MODEL_FEATURES ** -0.5, 0.109375),
        "value_up_weight": bell_draw(key_of[9], (ADAPTER_RANK, KEY_VALUE_HEADS * HEAD_SIZE), ADAPTER_RANK ** -0.5, 1.5),
        "output_gradient": bell_draw(own_keys[10], (NSEQ, SEQ, QUERY_HEADS * HEAD_SIZE), 4.0, 24.0, ((0, 16), (1, 2))),
    }


CAP = 50.0
QSCALE = 1.0 / 12.0
ADAPTER_NAME = 0.5
EPS = 1e-06

def normed_rows(values, gain):
    flt = values.astype(jnp.float32)
    meansq = lax.optimization_barrier(jnp.mean(flt * flt, axis=-1, keepdims=True))
    return (flt * lax.rsqrt(meansq + EPS) * gain.astype(jnp.float32)).astype(jnp.bfloat16)

def earlier_blocks(stack, distance):
    filler = jnp.zeros((distance,) + stack.shape[1:], stack.dtype)
    return jnp.concatenate([filler, stack[:stack.shape[0] - distance]], 0)

def later_blocks(stack, distance):
    filler = jnp.zeros((distance,) + stack.shape[1:], stack.dtype)
    return jnp.concatenate([stack[distance:], filler], 0)

def attend_block(operands):
    q_blk, k_blk, v_blk, g_blk, mask = operands
    qf = q_blk.astype(jnp.float32)
    kf = k_blk.astype(jnp.float32)
    vf = v_blk.astype(jnp.float32)
    gf = g_blk.astype(jnp.float32)
    s = jnp.einsum('ikgd,jkd->kgij', qf, kf) * QSCALE
    t = jnp.tanh(s / CAP)
    capped = CAP * t
    expo = jnp.where(mask[None, None], jnp.exp(capped), jnp.float32(0.0))
    weights = expo / lax.optimization_barrier(jnp.sum(expo, axis=-1, keepdims=True))
    weights16 = weights.astype(jnp.bfloat16).astype(jnp.float32)
    attended = jnp.einsum('kgij,jkd->ikgd', weights16, vf)
    dweight = jnp.einsum('ikgd,jkd->kgij', gf, vf)
    delta = jnp.einsum('ikgd,ikgd->kgi', gf, attended)
    dscore = (weights * (dweight - delta[..., None]) * (1.0 - t * t) * QSCALE).astype(jnp.bfloat16)
    query_gradient = jnp.einsum('kgij,jkd->ikgd', dscore.astype(jnp.float32), kf).astype(jnp.bfloat16)
    value_gradient = jnp.einsum('kgij,ikgd->jkd', weights16, gf)
    return (query_gradient, value_gradient)

def reference(tokens, trace_index, input_norm_scale, query_weight, key_weight, value_weight, query_down_weight, query_up_weight, value_down_weight, value_up_weight, output_gradient):
    row_slice = NSEQ * SEQ
    head_group = QUERY_HEADS // KEY_VALUE_HEADS
    window_width = TOK_DEV
    block_list = row_slice // window_width
    per_seq = SEQ // window_width
    normalized_input = normed_rows(tokens.reshape(row_slice, MODEL_FEATURES), input_norm_scale)
    query_reduced = jnp.dot(normalized_input, query_down_weight, preferred_element_type=jnp.float32).astype(jnp.bfloat16)
    value_reduced = jnp.dot(normalized_input, value_down_weight, preferred_element_type=jnp.float32).astype(jnp.bfloat16)
    query_matrix = (jnp.dot(normalized_input, query_weight, preferred_element_type=jnp.float32) + ADAPTER_NAME * jnp.dot(query_reduced, query_up_weight, preferred_element_type=jnp.float32)).astype(jnp.bfloat16)
    key = jnp.dot(normalized_input, key_weight, preferred_element_type=jnp.float32).astype(jnp.bfloat16)
    value_matrix = (jnp.dot(normalized_input, value_weight, preferred_element_type=jnp.float32) + ADAPTER_NAME * jnp.dot(value_reduced, value_up_weight, preferred_element_type=jnp.float32)).astype(jnp.bfloat16)
    query_blocks = query_matrix.reshape(block_list, window_width, KEY_VALUE_HEADS, head_group, HEAD_SIZE)
    gradient_blocks = output_gradient.reshape(block_list, window_width, KEY_VALUE_HEADS, head_group, HEAD_SIZE)
    key_blocks = key.reshape(block_list, window_width, KEY_VALUE_HEADS, HEAD_SIZE)
    value_blocks = value_matrix.reshape(block_list, window_width, KEY_VALUE_HEADS, HEAD_SIZE)
    k_triples = jnp.concatenate([earlier_blocks(key_blocks, 2), earlier_blocks(key_blocks, 1), key_blocks], 1)
    v_triples = jnp.concatenate([earlier_blocks(value_blocks, 2), earlier_blocks(value_blocks, 1), value_blocks], 1)
    seg_blocks = trace_index.reshape(block_list, window_width)
    seg_keys = jnp.concatenate([earlier_blocks(seg_blocks, 2), earlier_blocks(seg_blocks, 1), seg_blocks], 1)
    pos_q = jnp.arange(window_width, dtype=jnp.int32)[:, None]
    pos_k = jnp.arange(3 * window_width, dtype=jnp.int32)[None, :]
    band = (pos_k > pos_q) & (pos_k <= pos_q + WINDOW)
    offset = jnp.arange(block_list, dtype=jnp.int32) % per_seq
    valid = (pos_k >= 2 * window_width)[None] | (pos_k >= window_width)[None] & (offset >= 1)[:, None, None] | (offset >= 2)[:, None, None]
    mask = band[None] & (seg_keys[:, None, :] == seg_blocks[:, :, None]) & valid
    query_gradient, dvalue_triples = lax.map(attend_block, (query_blocks, k_triples, v_triples, gradient_blocks, mask))
    query_gradient = query_gradient.reshape(row_slice, QUERY_HEADS * HEAD_SIZE)
    self_portion = dvalue_triples[:, 2 * window_width:]
    nearby_portion = later_blocks(dvalue_triples[:, window_width:2 * window_width], 1)
    distant_portion = later_blocks(dvalue_triples[:, :window_width], 2)
    value_gradient = (self_portion + nearby_portion + distant_portion).reshape(row_slice, KEY_VALUE_HEADS * HEAD_SIZE)
    query_backward = jnp.dot(query_gradient, query_up_weight.T, preferred_element_type=jnp.float32).astype(jnp.bfloat16)
    value_backward = jnp.dot(value_gradient, value_up_weight.astype(jnp.float32).T, precision=lax.Precision.HIGHEST)
    coefficient = ADAPTER_NAME / math.sqrt(TOKEN_COUNT)
    grad_a_query = jnp.dot(normalized_input.T, query_backward, preferred_element_type=jnp.float32) * coefficient
    grad_b_query = jnp.dot(query_reduced.T, query_gradient, preferred_element_type=jnp.float32) * coefficient
    grad_a_value = jnp.dot(normalized_input.astype(jnp.float32).T, value_backward, precision=lax.Precision.HIGHEST) * coefficient
    grad_b_value = jnp.dot(value_reduced.astype(jnp.float32).T, value_gradient, precision=lax.Precision.HIGHEST) * coefficient
    return (grad_a_query, grad_b_query, grad_a_value, grad_b_value)
```

```python
import functools
import math

import jax
import jax.numpy as jnp
from jax import lax
from jax.experimental import pallas as pl
from jax.experimental.pallas import tpu as pltpu
from jax.sharding import PartitionSpec as P

HEAD_SIZE = 128


CAP = 50.0
QSCALE = 1.0 / 12.0
ADAPTER_NAME = 0.5
EPS = 1e-06


def shifted(value, axis, by):
    devices = lax.axis_size(axis)
    pairs = [(i, i + by) for i in range(devices) if 0 <= i + by < devices]
    return lax.ppermute(value, axis, pairs)


def normed_rows(values, gain):
    flt = values.astype(jnp.float32)
    meansq = jnp.mean(flt * flt, axis=-1, keepdims=True)
    return (flt * lax.rsqrt(meansq + EPS) * gain.astype(jnp.float32)).astype(jnp.bfloat16)


def add_rows(left, piece):
    return jnp.dot(left, piece, preferred_element_type=jnp.float32)


def attend_head(operands, mask):
    q_head, k_head, v_head, g_head = operands
    s = jnp.einsum("igd,jd->gij", q_head, k_head, preferred_element_type=jnp.float32) * QSCALE
    t = jnp.tanh(s / CAP)
    capped = CAP * t
    expo = jnp.where(mask[None], jnp.exp(capped), jnp.float32(0.0))
    weights = expo / jnp.sum(expo, axis=-1, keepdims=True)
    weights16 = weights.astype(jnp.bfloat16)
    attended = jnp.einsum("gij,jd->igd", weights16, v_head, preferred_element_type=jnp.float32)
    dweight = jnp.einsum("igd,jd->gij", g_head, v_head, preferred_element_type=jnp.float32)
    delta = jnp.sum(g_head.astype(jnp.float32) * attended, axis=-1).T
    dscore = (weights * (dweight - delta[..., None]) * (1.0 - t * t) * QSCALE).astype(jnp.bfloat16)
    query_gradient = jnp.einsum(
        "gij,jd->igd", dscore, k_head, preferred_element_type=jnp.float32
    ).astype(jnp.bfloat16)
    value_gradient = jnp.einsum(
        "gij,igd->jd", weights16, g_head, preferred_element_type=jnp.float32
    )
    return (query_gradient, value_gradient)


def partial_attend(mask):

    def run_head(operands):
        return attend_head(operands, mask)

    return run_head


def on_device(
    tokens,
    trace_index,
    input_norm_scale,
    query_weight,
    key_weight,
    value_weight,
    query_down_weight,
    query_up_weight,
    value_down_weight,
    value_up_weight,
    output_gradient,
):
    window_width = tokens.shape[1]
    feats = tokens.shape[2]
    heads_kv = key_weight.shape[1] // HEAD_SIZE
    heads_q = query_weight.shape[1] // HEAD_SIZE
    head_group = heads_q // heads_kv
    normalized_input = normed_rows(tokens.reshape(window_width, feats), input_norm_scale)
    seg_own = trace_index.reshape(window_width).astype(jnp.bfloat16)
    seg_parts = []

    def add_keyval(piece):
        return add_rows(normalized_input, piece)

    query_frozen = add_rows(
        normalized_input, lax.all_gather(query_weight, "fsdp", axis=0, tiled=True)
    )
    k_base = add_keyval(lax.all_gather(key_weight, "fsdp", axis=0, tiled=True))
    value_frozen = add_keyval(lax.all_gather(value_weight, "fsdp", axis=0, tiled=True))
    query_reduced = jnp.dot(
        normalized_input, query_down_weight, preferred_element_type=jnp.float32
    ).astype(jnp.bfloat16)
    reduced_rows = jnp.dot(
        normalized_input, value_down_weight, preferred_element_type=jnp.float32
    ).astype(jnp.bfloat16)
    query_matrix = (
        query_frozen
        + ADAPTER_NAME * jnp.dot(query_reduced, query_up_weight, preferred_element_type=jnp.float32)
    ).astype(jnp.bfloat16)
    key_rows = k_base.astype(jnp.bfloat16)
    value_rows = (
        value_frozen
        + ADAPTER_NAME * jnp.dot(reduced_rows, value_up_weight, preferred_element_type=jnp.float32)
    ).astype(jnp.bfloat16)
    key_parts = []
    value_parts = []
    for distance in (2, 1):
        key_prev, value_prev, seg_prev = shifted((key_rows, value_rows, seg_own), "ctx", distance)
        key_parts.append(key_prev)
        value_parts.append(value_prev)
        seg_parts.append(seg_prev)
    keys_all = jnp.concatenate(key_parts + [key_rows], 0)
    values_all = jnp.concatenate(value_parts + [value_rows], 0)
    seg_keys = jnp.concatenate(seg_parts + [seg_own], 0)
    pos_q = jnp.arange(window_width, dtype=jnp.int32)[:, None]
    pos_k = jnp.arange(3 * window_width, dtype=jnp.int32)[None, :]
    position = lax.axis_index("ctx")
    mask = (
        (pos_k > pos_q)
        & (pos_k <= pos_q + 2 * window_width)
        & (seg_keys[None, :] == seg_own[:, None])
    )
    mask = mask & (
        (pos_k >= 2 * window_width) | (pos_k >= window_width) & (position >= 1) | (position >= 2)
    )
    q_heads = jnp.moveaxis(
        query_matrix.reshape(window_width, heads_kv, head_group, HEAD_SIZE), 1, 0
    )
    g_heads = jnp.moveaxis(
        output_gradient.reshape(window_width, heads_kv, head_group, HEAD_SIZE), 1, 0
    )
    k_heads = jnp.moveaxis(keys_all.reshape(3 * window_width, heads_kv, HEAD_SIZE), 1, 0)
    v_heads = jnp.moveaxis(values_all.reshape(3 * window_width, heads_kv, HEAD_SIZE), 1, 0)
    dquery_heads, dvalue_heads = lax.map(partial_attend(mask), (q_heads, k_heads, v_heads, g_heads))
    query_gradient = jnp.moveaxis(dquery_heads, 0, 1).reshape(window_width, heads_q * HEAD_SIZE)
    dvalue_triple = jnp.moveaxis(dvalue_heads, 0, 1).reshape(3 * window_width, heads_kv * HEAD_SIZE)
    value_gradient = dvalue_triple[2 * window_width :]
    for distance in (1, 2):
        begin = (2 - distance) * window_width
        value_gradient = value_gradient + shifted(
            dvalue_triple[begin : begin + window_width], "ctx", -distance
        )
    query_backward = jnp.dot(
        query_gradient, query_up_weight.T, preferred_element_type=jnp.float32
    ).astype(jnp.bfloat16)
    value_backward = jnp.dot(
        value_gradient, value_up_weight.astype(jnp.float32).T, precision=lax.Precision.HIGHEST
    )
    part_aq = jnp.dot(normalized_input.T, query_backward, preferred_element_type=jnp.float32)
    part_bq = jnp.dot(query_reduced.T, query_gradient, preferred_element_type=jnp.float32)
    part_av = jnp.dot(
        normalized_input.astype(jnp.float32).T, value_backward, precision=lax.Precision.HIGHEST
    )
    part_bv = jnp.dot(
        reduced_rows.astype(jnp.float32).T, value_gradient, precision=lax.Precision.HIGHEST
    )
    sum_aq, sum_bq, sum_av, sum_bv = lax.psum((part_aq, part_bq, part_av, part_bv), ("ctx", "fsdp"))
    token_total = lax.axis_size("ctx") * lax.axis_size("fsdp") * window_width
    coefficient = ADAPTER_NAME / math.sqrt(token_total)
    return (sum_aq * coefficient, sum_bq * coefficient, sum_av * coefficient, sum_bv * coefficient)


F32 = jnp.float32
BF16 = jnp.bfloat16
PLANE = 8


def dot(a, b, dims=((1,), (0,))):
    return lax.dot_general(a, b, (dims, ((), ())), preferred_element_type=F32)


def plane_kernel(
    chain, coefficient,
    norm, seg, wq, wk, wv, qd, qu, vd, vu, grad,
    out_aq, out_bq, out_av, out_bv,
    N, W, G, SG, acc, DQ, DV, LQ, LV, A, RA, S, RS, T, OUT,
    local_sem, w_send, w_recv, t_send, t_recv, g_send, g_recv, s_send, s_recv,
    up_send, up_recv, down_send, down_recv,
    r1_send, r1_recv, r2_send, r2_recv, r3_send, r3_recv,
):
    x = lax.axis_index("ctx")
    f = lax.axis_index("fsdp")
    z = f // 4
    y = (f // 2) % 2
    c = f % 2
    tok, feats = norm.shape
    rows = wq.shape[0]
    qcols = wq.shape[1] // PLANE
    kcols = wk.shape[1] // PLANE
    piece = feats // PLANE
    plane_rows = 4 * rows
    seq = 2 * tok

    def coords(r):
        px = 1 - x if r & 4 else x
        py = 1 - y if r & 2 else y
        pc = 1 - c if r & 1 else c
        return px, py, pc

    def head_of(r):
        px, py, pc = coords(r)
        return (px * 2 + py) * 2 + pc

    def peer(r):
        px, py, pc = coords(r)
        return {"ctx": px, "fsdp": (z * 2 + py) * 2 + pc}

    def above(pz):
        return {"ctx": x, "fsdp": (pz * 2 + y) * 2 + c}

    def tok_rows(r):
        px, py, pc = coords(r)
        return pl.ds(pl.multiple_of(((py * 2 + pc) * 2 + px) * tok, tok), tok)

    def remote(src, dst, send, recv, device):
        return pltpu.make_async_remote_copy(
            src_ref=src, dst_ref=dst, send_sem=send, recv_sem=recv,
            device_id=device, device_id_type=pl.DeviceIdType.MESH,
        )

    barrier = pltpu.get_barrier_semaphore()
    for r in range(1, PLANE):
        pl.semaphore_signal(barrier, inc=1, device_id=peer(r), device_id_type=pl.DeviceIdType.MESH)
    for d in range(1, chain):
        pl.semaphore_signal(
            barrier, inc=1, device_id=above((z + d) % chain), device_id_type=pl.DeviceIdType.MESH
        )

    def w_rows(r):
        px, py, pc = coords(r)
        return pl.ds(pl.multiple_of(((z * 2 + py) * 2 + pc) * rows, rows), rows)

    def w_parts(r):
        h = head_of(r)
        own = w_rows(0)
        return (
            (wq.at[:, pl.ds(pl.multiple_of(h * qcols, qcols), qcols)], W.at[own, pl.ds(0, qcols)]),
            (wk.at[:, pl.ds(pl.multiple_of(h * kcols, kcols), kcols)], W.at[own, pl.ds(qcols, kcols)]),
            (wv.at[:, pl.ds(pl.multiple_of(h * kcols, kcols), kcols)], W.at[own, pl.ds(qcols + kcols, kcols)]),
        )

    def g_cols(r):
        h = head_of(r)
        return grad.at[:, pl.ds(pl.multiple_of(h * qcols, qcols), qcols)]

    local = [pltpu.make_async_copy(a, b, local_sem.at[i]) for i, (a, b) in enumerate(w_parts(0))]
    local.append(pltpu.make_async_copy(norm, N.at[tok_rows(0)], local_sem.at[3]))
    local.append(pltpu.make_async_copy(g_cols(0), G.at[tok_rows(0)], local_sem.at[4]))
    local.append(pltpu.make_async_copy(seg, SG.at[tok_rows(0)], local_sem.at[5]))
    for copy in local:
        copy.start()
    pl.semaphore_wait(barrier, PLANE - 1 + chain - 1)

    w_copies = {}
    for r in (1, 2, 3):
        w_copies[r] = [
            remote(a, b, w_send.at[r, i], w_recv.at[r, i], peer(r)) for i, (a, b) in enumerate(w_parts(r))
        ]
        for copy in w_copies[r]:
            copy.start()
    t_copies = {}
    for r in (2, 4, 1):
        t_copies[r] = remote(norm, N.at[tok_rows(0)], t_send.at[r], t_recv.at[r], peer(r))
        t_copies[r].start()
    g_copies = {}
    s_copies = {}
    for r in range(1, PLANE):
        g_copies[r] = remote(g_cols(r), G.at[tok_rows(0)], g_send.at[r], g_recv.at[r], peer(r))
        s_copies[r] = remote(seg, SG.at[tok_rows(0)], s_send.at[r], s_recv.at[r], peer(r))

    def half_rows(plane, half):
        py = y if half == 0 else 1 - y
        return pl.ds(pl.multiple_of((plane * 4 + py * 2) * rows, 2 * rows), 2 * rows)

    def up_copy(t, half):
        at = W.at[half_rows(z - t, half)]
        return remote(at, at, up_send.at[t, half], up_recv.at[t, half], above(z + 1))

    def down_copy(t, half):
        at = W.at[half_rows(z + t, half)]
        return remote(at, at, down_send.at[t, half], down_recv.at[t, half], above(z - 1))

    def up_arrival(t, half):
        at = W.at[half_rows(z - 1 - t, half)]
        return remote(at, at, up_send.at[t, half], up_recv.at[t, half], above(z - 1))

    def down_arrival(t, half):
        at = W.at[half_rows(z + 1 + t, half)]
        return remote(at, at, down_send.at[t, half], down_recv.at[t, half], above(z + 1))

    def has_up(t):
        return (z < chain - 1) & (z - t >= 0)

    def has_down(t):
        return (z > 0) & (z + t <= chain - 1)

    def send_chain(t, half):
        @pl.when(has_up(t))
        def _():
            up_copy(t, half).start()

        @pl.when(has_down(t))
        def _():
            down_copy(t, half).start()

    def recv_chain(t, half):
        @pl.when(z - 1 - t >= 0)
        def _():
            up_arrival(t, half).wait_recv()

        @pl.when(z + 1 + t <= chain - 1)
        def _():
            down_arrival(t, half).wait_recv()

    def forward_token(r_mine, r_there, hop):
        at = N.at[tok_rows(r_mine)]
        t_copies[r_there] = remote(at, at, t_send.at[r_there], t_recv.at[r_there], peer(hop))
        t_copies[r_there].start()

    def wait_token(r):
        at = N.at[tok_rows(r)]
        remote(at, at, t_send.at[r], t_recv.at[r], peer(1)).wait_recv()

    def wait_weight(r):
        at = w_rows(r)
        for i, (lo, width) in enumerate(((0, qcols), (qcols, kcols), (qcols + kcols, kcols))):
            ref = W.at[at, pl.ds(lo, width)]
            remote(ref, ref, w_send.at[r, i], w_recv.at[r, i], peer(r)).wait_recv()

    for i in range(3):
        local[i].wait()
    wait_weight(1)
    send_chain(0, 0)
    wait_weight(2)
    wait_weight(3)
    send_chain(0, 1)
    for r in range(1, PLANE):
        g_copies[r].start()
        s_copies[r].start()
    wait_token(4)
    forward_token(4, 5, 1)
    if chain > 1:
        for half in range(2):
            recv_chain(0, half)
            if chain > 2:
                send_chain(1, half)
    wait_token(2)
    forward_token(2, 6, 4)
    forward_token(2, 3, 1)
    for t in range(1, chain - 2):
        for half in range(2):
            recv_chain(t, half)
            send_chain(t + 1, half)
    wait_token(6)
    forward_token(6, 7, 1)
    local[3].wait()
    for r in (1, 5, 3, 7):
        wait_token(r)

    tiles = PLANE * tok // seq

    @pl.loop(0, tiles)
    def _(i):
        at = pl.ds(pl.multiple_of(i * seq, seq), seq)
        block = N[at, :]
        LQ[at, :] = dot(block, qd[...]).astype(BF16)
        LV[at, :] = dot(block, vd[...]).astype(BF16)
        acc[at, :] = jnp.zeros((seq, acc.shape[1]), F32)

    def add_plane(plane):
        weights = W.at[pl.ds(pl.multiple_of(plane * plane_rows, plane_rows), plane_rows)]
        columns = pl.ds(pl.multiple_of(plane * plane_rows, plane_rows), plane_rows)

        @pl.loop(0, tiles)
        def _(i):
            at = pl.ds(pl.multiple_of(i * seq, seq), seq)
            acc[at, :] += dot(N[at, columns], weights[...])

    add_plane(z)
    for t in range(chain - 1):
        if t == chain - 2 and t > 0:
            for half in range(2):
                recv_chain(t, half)

        @pl.when(z - 1 - t >= 0)
        def _():
            add_plane(z - 1 - t)

        @pl.when(z + 1 + t <= chain - 1)
        def _():
            add_plane(z + 1 + t)

    h = head_of(0)
    qu_own = qu[:, pl.ds(pl.multiple_of(h * qcols, qcols), qcols)]
    vu_own = vu[:, pl.ds(pl.multiple_of(h * kcols, kcols), kcols)]
    local[4].wait()
    local[5].wait()
    for r in range(1, PLANE):
        at = G.at[tok_rows(r)]
        remote(at, at, g_send.at[r], g_recv.at[r], peer(r)).wait_recv()
        at = SG.at[tok_rows(r)]
        remote(at, at, s_send.at[r], s_recv.at[r], peer(r)).wait_recv()

    pos_i = lax.broadcasted_iota(jnp.int32, (seq, seq), 0)
    pos_j = lax.broadcasted_iota(jnp.int32, (seq, seq), 1)
    band = (pos_j <= pos_i) & (pos_j > pos_i - 2 * tok)

    @pl.loop(0, tiles)
    def _(i):
        at = pl.ds(pl.multiple_of(i * seq, seq), seq)
        q_all = (acc[at, 0:qcols] + ADAPTER_NAME * dot(LQ[at, :], qu_own)).astype(BF16)
        k = acc[at, qcols:qcols + kcols].astype(BF16)
        v = (acc[at, qcols + kcols:] + ADAPTER_NAME * dot(LV[at, :], vu_own)).astype(BF16)
        g_all = G[at, :]
        own = SG[at, :].astype(F32)
        across = jnp.concatenate([own] * (seq // own.shape[1]), axis=1)
        along = jnp.concatenate([own[:tok].T, own[tok:].T], axis=1)[0:1, :]
        mask = band & (across == along)
        dv = jnp.zeros((seq, kcols), F32)
        for n in range(qcols // kcols):
            q = q_all[:, n * kcols:(n + 1) * kcols]
            g = g_all[:, n * kcols:(n + 1) * kcols]
            s = dot(q, k, ((1,), (1,))) * QSCALE
            t = jnp.tanh(s / CAP)
            expo = jnp.where(mask, jnp.exp(CAP * t), 0.0)
            weights = expo / jnp.sum(expo, axis=-1, keepdims=True)
            weights16 = weights.astype(BF16)
            attended = dot(weights16, v)
            dweight = dot(g, v, ((1,), (1,)))
            delta = jnp.sum(g.astype(F32) * attended, axis=-1, keepdims=True)
            dscore = (weights * (dweight - delta) * (1.0 - t * t) * QSCALE).astype(BF16)
            DQ[at, n * kcols:(n + 1) * kcols] = dot(dscore, k).astype(BF16)
            dv = dv + dot(weights16, g, ((0,), (0,)))
        DV[at, :] = dv.astype(BF16)

    pull_q = dot(qu_own, DQ[...], ((1,), (1,))).astype(BF16)
    pull_v = dot(vu_own, DV[...], ((1,), (1,))).astype(BF16)
    pull = jnp.concatenate([pull_q, pull_v], axis=0)
    ranks = pull.shape[0]
    half_rank = ranks // 2
    r1_copies = []
    for r in (7, 6, 5, 4, 3, 2, 1, 0):
        columns = pl.ds(pl.multiple_of(head_of(r) * piece, piece), piece)
        A[r] = dot(pull, N[:, columns])
        if r > 0:
            copy = remote(A.at[r], RA.at[r], r1_send.at[r], r1_recv.at[r], peer(r))
            copy.start()
            r1_copies.append(copy)
    S[ranks:, 0:qcols] = dot(LQ[...], DQ[...], ((0,), (0,)))
    S[ranks:, qcols:qcols + kcols] = dot(LV[...], DV[...], ((0,), (0,)))
    for copy in r1_copies:
        copy.wait_recv()
    total = A[0]
    for r in range(1, PLANE):
        total = total + RA[r]
    S[0:ranks, :] = total
    r2_copies = []
    for d in range(1, chain):
        copy = remote(S, RS.at[d], r2_send.at[d], r2_recv.at[d], above((z + d) % chain))
        copy.start()
        r2_copies.append(copy)
    for copy in r2_copies:
        copy.wait_recv()
    total = S[...]
    for d in range(1, chain):
        total = total + RS[d]
    total = total * coefficient
    T[...] = total
    r3_copies = []
    for r in (7, 6, 5, 4, 3, 2, 1):
        copy = remote(T, OUT.at[r], r3_send.at[r], r3_recv.at[r], peer(r))
        copy.start()
        r3_copies.append(copy)

    def put(r, value):
        hp = head_of(r)
        fcols = pl.ds(pl.multiple_of(hp * piece, piece), piece)
        out_aq[:, fcols] = value[0:half_rank]
        out_av[:, fcols] = value[half_rank:ranks]
        out_bq[:, pl.ds(pl.multiple_of(hp * qcols, qcols), qcols)] = value[ranks:, 0:qcols]
        out_bv[:, pl.ds(pl.multiple_of(hp * kcols, kcols), kcols)] = value[ranks:, qcols:qcols + kcols]

    put(0, total)
    for i, r in enumerate((7, 6, 5, 4, 3, 2, 1)):
        r3_copies[i].wait_recv()
    for r in range(1, PLANE):
        put(r, OUT[r])

    for r in (1, 2, 3):
        for copy in w_copies[r]:
            copy.wait_send()
    for r in range(1, PLANE):
        t_copies[r].wait_send()
        g_copies[r].wait_send()
        s_copies[r].wait_send()
    for t in range(chain - 1):
        for half in range(2):
            @pl.when(has_up(t))
            def _():
                up_copy(t, half).wait_send()

            @pl.when(has_down(t))
            def _():
                down_copy(t, half).wait_send()
    for copy in r1_copies + r2_copies + r3_copies:
        copy.wait_send()


def on_plane(
    tokens,
    trace_index,
    input_norm_scale,
    query_weight,
    key_weight,
    value_weight,
    query_down_weight,
    query_up_weight,
    value_down_weight,
    value_up_weight,
    output_gradient,
):
    tok = tokens.shape[1]
    feats = tokens.shape[2]
    fsdp = lax.axis_size("fsdp")
    chain = fsdp // 4
    ranks = query_down_weight.shape[1]
    qcols = query_weight.shape[1] // PLANE
    kcols = key_weight.shape[1] // PLANE
    columns = qcols + 2 * kcols
    piece = feats // PLANE
    many = PLANE * tok
    normed = normed_rows(tokens.reshape(tok, feats), input_norm_scale)
    seg = jnp.broadcast_to(trace_index.reshape(tok, 1), (tok, 128)).astype(BF16)
    token_total = lax.axis_size("ctx") * fsdp * tok
    coefficient = ADAPTER_NAME / math.sqrt(token_total)
    hbm = pl.BlockSpec(memory_space=pl.ANY)
    vmem = pl.BlockSpec(memory_space=pltpu.VMEM)
    dma = pltpu.SemaphoreType.DMA
    steps = max(chain - 1, 1)
    aq, bq, av, bv = pl.pallas_call(
        functools.partial(plane_kernel, chain, coefficient),
        out_shape=(
            jax.ShapeDtypeStruct((ranks, feats), F32),
            jax.ShapeDtypeStruct((ranks, query_weight.shape[1]), F32),
            jax.ShapeDtypeStruct((ranks, feats), F32),
            jax.ShapeDtypeStruct((ranks, value_weight.shape[1]), F32),
        ),
        in_specs=[hbm, hbm, hbm, hbm, hbm, vmem, vmem, vmem, vmem, hbm],
        out_specs=(vmem, vmem, vmem, vmem),
        scratch_shapes=[
            pltpu.VMEM((many, feats), BF16),
            pltpu.VMEM((feats, columns), BF16),
            pltpu.VMEM((many, qcols), BF16),
            pltpu.VMEM((many, 128), BF16),
            pltpu.VMEM((many, columns), F32),
            pltpu.VMEM((many, qcols), BF16),
            pltpu.VMEM((many, kcols), BF16),
            pltpu.VMEM((many, ranks), BF16),
            pltpu.VMEM((many, ranks), BF16),
            pltpu.VMEM((PLANE, 2 * ranks, piece), F32),
            pltpu.VMEM((PLANE, 2 * ranks, piece), F32),
            pltpu.VMEM((3 * ranks, piece), F32),
            pltpu.VMEM((chain, 3 * ranks, piece), F32),
            pltpu.VMEM((3 * ranks, piece), F32),
            pltpu.VMEM((PLANE, 3 * ranks, piece), F32),
            dma((6,)),
            dma((4, 3)), dma((4, 3)),
            dma((8,)), dma((8,)), dma((8,)), dma((8,)), dma((8,)), dma((8,)),
            dma((steps, 2)), dma((steps, 2)), dma((steps, 2)), dma((steps, 2)),
            dma((8,)), dma((8,)), dma((max(chain, 2),)), dma((max(chain, 2),)), dma((8,)), dma((8,)),
        ],
        compiler_params=pltpu.CompilerParams(
            collective_id=0, has_side_effects=True, vmem_limit_bytes=56 * 1024 * 1024
        ),
    )(
        normed, seg, query_weight, key_weight, value_weight,
        query_down_weight, query_up_weight, value_down_weight, value_up_weight,
        output_gradient.reshape(tok, output_gradient.shape[2]),
    )
    return (aq.T, bq, av.T, bv)


def solution(mesh):
    shape = mesh.shape
    planes = shape["groups"] == 1 and shape["ctx"] == 2 and shape["fsdp"] % 4 == 0 and shape["fsdp"] > 8
    return jax.shard_map(
        on_plane if planes else on_device,
        mesh=mesh,
        in_specs=(
            P(("groups", "fsdp"), "ctx", None),
            P(("groups", "fsdp"), "ctx"),
            P(),
            P("fsdp", None),
            P("fsdp", None),
            P("fsdp", None),
            P(),
            P(),
            P(),
            P(),
            P(("groups", "fsdp"), "ctx", None),
        ),
        out_specs=(P("groups", None), P("groups", None), P("groups", None), P("groups", None)),
        check_vma=False,
    )
```

```python
import functools
import math

import jax
import jax.numpy as jnp
from jax import lax
from jax.experimental import pallas as pl
from jax.experimental.pallas import tpu as pltpu
from jax.sharding import PartitionSpec as P

HEAD_SIZE = 128


CAP = 50.0
QSCALE = 1.0 / 12.0
ADAPTER_NAME = 0.5
EPS = 1e-06


def shifted(value, axis, by):
    devices = lax.axis_size(axis)
    pairs = [(i, i + by) for i in range(devices) if 0 <= i + by < devices]
    return lax.ppermute(value, axis, pairs)


def normed_rows(values, gain):
    flt = values.astype(jnp.float32)
    meansq = jnp.mean(flt * flt, axis=-1, keepdims=True)
    return (flt * lax.rsqrt(meansq + EPS) * gain.astype(jnp.float32)).astype(jnp.bfloat16)


def add_rows(left, piece):
    return jnp.dot(left, piece, preferred_element_type=jnp.float32)


def attend_head(operands, mask):
    q_head, k_head, v_head, g_head = operands
    s = jnp.einsum("igd,jd->gij", q_head, k_head, preferred_element_type=jnp.float32) * QSCALE
    t = jnp.tanh(s / CAP)
    capped = CAP * t
    expo = jnp.where(mask[None], jnp.exp(capped), jnp.float32(0.0))
    weights = expo / jnp.sum(expo, axis=-1, keepdims=True)
    weights16 = weights.astype(jnp.bfloat16)
    attended = jnp.einsum("gij,jd->igd", weights16, v_head, preferred_element_type=jnp.float32)
    dweight = jnp.einsum("igd,jd->gij", g_head, v_head, preferred_element_type=jnp.float32)
    delta = jnp.sum(g_head.astype(jnp.float32) * attended, axis=-1).T
    dscore = (weights * (dweight - delta[..., None]) * (1.0 - t * t) * QSCALE).astype(jnp.bfloat16)
    query_gradient = jnp.einsum(
        "gij,jd->igd", dscore, k_head, preferred_element_type=jnp.float32
    ).astype(jnp.bfloat16)
    value_gradient = jnp.einsum(
        "gij,igd->jd", weights16, g_head, preferred_element_type=jnp.float32
    )
    return (query_gradient, value_gradient)


def partial_attend(mask):

    def run_head(operands):
        return attend_head(operands, mask)

    return run_head


def on_device(
    tokens,
    trace_index,
    input_norm_scale,
    query_weight,
    key_weight,
    value_weight,
    query_down_weight,
    query_up_weight,
    value_down_weight,
    value_up_weight,
    output_gradient,
):
    window_width = tokens.shape[1]
    feats = tokens.shape[2]
    heads_kv = key_weight.shape[1] // HEAD_SIZE
    heads_q = query_weight.shape[1] // HEAD_SIZE
    head_group = heads_q // heads_kv
    normalized_input = normed_rows(tokens.reshape(window_width, feats), input_norm_scale)
    seg_own = trace_index.reshape(window_width).astype(jnp.bfloat16)
    seg_parts = []

    def add_keyval(piece):
        return add_rows(normalized_input, piece)

    query_frozen = add_rows(
        normalized_input, lax.all_gather(query_weight, "fsdp", axis=0, tiled=True)
    )
    k_base = add_keyval(lax.all_gather(key_weight, "fsdp", axis=0, tiled=True))
    value_frozen = add_keyval(lax.all_gather(value_weight, "fsdp", axis=0, tiled=True))
    query_reduced = jnp.dot(
        normalized_input, query_down_weight, preferred_element_type=jnp.float32
    ).astype(jnp.bfloat16)
    reduced_rows = jnp.dot(
        normalized_input, value_down_weight, preferred_element_type=jnp.float32
    ).astype(jnp.bfloat16)
    query_matrix = (
        query_frozen
        + ADAPTER_NAME * jnp.dot(query_reduced, query_up_weight, preferred_element_type=jnp.float32)
    ).astype(jnp.bfloat16)
    key_rows = k_base.astype(jnp.bfloat16)
    value_rows = (
        value_frozen
        + ADAPTER_NAME * jnp.dot(reduced_rows, value_up_weight, preferred_element_type=jnp.float32)
    ).astype(jnp.bfloat16)
    key_parts = []
    value_parts = []
    for distance in (2, 1):
        key_prev, value_prev, seg_prev = shifted((key_rows, value_rows, seg_own), "ctx", distance)
        key_parts.append(key_prev)
        value_parts.append(value_prev)
        seg_parts.append(seg_prev)
    keys_all = jnp.concatenate(key_parts + [key_rows], 0)
    values_all = jnp.concatenate(value_parts + [value_rows], 0)
    seg_keys = jnp.concatenate(seg_parts + [seg_own], 0)
    pos_q = jnp.arange(window_width, dtype=jnp.int32)[:, None]
    pos_k = jnp.arange(3 * window_width, dtype=jnp.int32)[None, :]
    position = lax.axis_index("ctx")
    mask = (
        (pos_k > pos_q)
        & (pos_k <= pos_q + 2 * window_width)
        & (seg_keys[None, :] == seg_own[:, None])
    )
    mask = mask & (
        (pos_k >= 2 * window_width) | (pos_k >= window_width) & (position >= 1) | (position >= 2)
    )
    q_heads = jnp.moveaxis(
        query_matrix.reshape(window_width, heads_kv, head_group, HEAD_SIZE), 1, 0
    )
    g_heads = jnp.moveaxis(
        output_gradient.reshape(window_width, heads_kv, head_group, HEAD_SIZE), 1, 0
    )
    k_heads = jnp.moveaxis(keys_all.reshape(3 * window_width, heads_kv, HEAD_SIZE), 1, 0)
    v_heads = jnp.moveaxis(values_all.reshape(3 * window_width, heads_kv, HEAD_SIZE), 1, 0)
    dquery_heads, dvalue_heads = lax.map(partial_attend(mask), (q_heads, k_heads, v_heads, g_heads))
    query_gradient = jnp.moveaxis(dquery_heads, 0, 1).reshape(window_width, heads_q * HEAD_SIZE)
    dvalue_triple = jnp.moveaxis(dvalue_heads, 0, 1).reshape(3 * window_width, heads_kv * HEAD_SIZE)
    value_gradient = dvalue_triple[2 * window_width :]
    for distance in (1, 2):
        begin = (2 - distance) * window_width
        value_gradient = value_gradient + shifted(
            dvalue_triple[begin : begin + window_width], "ctx", -distance
        )
    query_backward = jnp.dot(
        query_gradient, query_up_weight.T, preferred_element_type=jnp.float32
    ).astype(jnp.bfloat16)
    value_backward = jnp.dot(
        value_gradient, value_up_weight.astype(jnp.float32).T, precision=lax.Precision.HIGHEST
    )
    part_aq = jnp.dot(normalized_input.T, query_backward, preferred_element_type=jnp.float32)
    part_bq = jnp.dot(query_reduced.T, query_gradient, preferred_element_type=jnp.float32)
    part_av = jnp.dot(
        normalized_input.astype(jnp.float32).T, value_backward, precision=lax.Precision.HIGHEST
    )
    part_bv = jnp.dot(
        reduced_rows.astype(jnp.float32).T, value_gradient, precision=lax.Precision.HIGHEST
    )
    sum_aq, sum_bq, sum_av, sum_bv = lax.psum((part_aq, part_bq, part_av, part_bv), ("ctx", "fsdp"))
    token_total = lax.axis_size("ctx") * lax.axis_size("fsdp") * window_width
    coefficient = ADAPTER_NAME / math.sqrt(token_total)
    return (sum_aq * coefficient, sum_bq * coefficient, sum_av * coefficient, sum_bv * coefficient)


F32 = jnp.float32
BF16 = jnp.bfloat16
PLANE = 8


def dot(a, b, dims=((1,), (0,))):
    return lax.dot_general(a, b, (dims, ((), ())), preferred_element_type=F32)


def plane_kernel(
    chain, coefficient,
    raw, seg, gain, wq, wk, wv, qd, qu, vd, vu, grad,
    OUT,
    N, M, W, G, SG, acc, DQ, DV, LQ, LV, A, RA, RS, T,
    local_sem, w_send, w_recv, t_send, t_recv, g_send, g_recv, s_send, s_recv,
    up_send, up_recv, down_send, down_recv,
    r1_send, r1_recv, r2_send, r2_recv, r3_send, r3_recv,
):
    x = lax.axis_index("ctx")
    f = lax.axis_index("fsdp")
    z = f // 4
    y = (f // 2) % 2
    c = f % 2
    tok, feats = raw.shape
    rows = wq.shape[0]
    qcols = wq.shape[1] // PLANE
    kcols = wk.shape[1] // PLANE
    piece = feats // PLANE
    plane_rows = 4 * rows
    seq = 2 * tok

    def coords(r):
        px = 1 - x if r & 4 else x
        py = 1 - y if r & 2 else y
        pc = 1 - c if r & 1 else c
        return px, py, pc

    def head_of(r):
        px, py, pc = coords(r)
        return (px * 2 + py) * 2 + pc

    def peer(r):
        px, py, pc = coords(r)
        return {"ctx": px, "fsdp": (z * 2 + py) * 2 + pc}

    def above(pz):
        return {"ctx": x, "fsdp": (pz * 2 + y) * 2 + c}

    def tok_rows(r):
        px, py, pc = coords(r)
        return pl.ds(pl.multiple_of(((py * 2 + pc) * 2 + px) * tok, tok), tok)

    def tok_slot(r):
        px, py, pc = coords(r)
        return (py * 2 + pc) * 2 + px

    def tok_piece(r, part):
        px, py, pc = coords(r)
        if part is None:
            return tok_rows(r)
        begin = ((py * 2 + pc) * 2 + px) * tok + part * (tok // 2)
        return pl.ds(pl.multiple_of(begin, tok // 2), tok // 2)

    def remote(src, dst, send, recv, device):
        return pltpu.make_async_remote_copy(
            src_ref=src, dst_ref=dst, send_sem=send, recv_sem=recv,
            device_id=device, device_id_type=pl.DeviceIdType.MESH,
        )

    barrier = pltpu.get_barrier_semaphore()
    for r in range(1, PLANE):
        pl.semaphore_signal(barrier, inc=1, device_id=peer(r), device_id_type=pl.DeviceIdType.MESH)
    for d in range(1, chain):
        pl.semaphore_signal(
            barrier, inc=1, device_id=above((z + d) % chain), device_id_type=pl.DeviceIdType.MESH
        )

    def w_rows(r):
        px, py, pc = coords(r)
        return pl.ds(pl.multiple_of(((z * 2 + py) * 2 + pc) * rows, rows), rows)

    def w_parts(r):
        h = head_of(r)
        own = w_rows(0)
        return (
            (wq.at[:, pl.ds(pl.multiple_of(h * qcols, qcols), qcols)], W.at[own, pl.ds(0, qcols)]),
            (wk.at[:, pl.ds(pl.multiple_of(h * kcols, kcols), kcols)], W.at[own, pl.ds(qcols, kcols)]),
            (wv.at[:, pl.ds(pl.multiple_of(h * kcols, kcols), kcols)], W.at[own, pl.ds(qcols + kcols, kcols)]),
        )

    def g_cols(r):
        h = head_of(r)
        return grad.at[:, pl.ds(pl.multiple_of(h * qcols, qcols), qcols)]

    local = [pltpu.make_async_copy(a, b, local_sem.at[i]) for i, (a, b) in enumerate(w_parts(0))]
    local.append(pltpu.make_async_copy(raw, N.at[tok_rows(0)], local_sem.at[3]))
    local.append(pltpu.make_async_copy(g_cols(0), G.at[tok_rows(0)], local_sem.at[4]))
    local.append(pltpu.make_async_copy(seg, SG.at[tok_slot(0)], local_sem.at[5]))
    for copy in local:
        copy.start()
    pl.semaphore_wait(barrier, PLANE - 1 + chain - 1)

    w_copies = {}
    for r in (1, 2, 3):
        w_copies[r] = [
            remote(a, b, w_send.at[r, i], w_recv.at[r, i], peer(r)) for i, (a, b) in enumerate(w_parts(r))
        ]
        for copy in w_copies[r]:
            copy.start()
    t_copies = []

    def send_token(r_mine, r_there, hop, part=None):
        at = N.at[tok_piece(r_mine, part)]
        source = at
        if r_mine == 0:
            source = raw if part is None else raw.at[pl.ds(part * (tok // 2), tok // 2)]
        i = part or 0
        copy = remote(source, at, t_send.at[r_there, i], t_recv.at[r_there, i], peer(hop))
        copy.start()
        t_copies.append(copy)

    send_token(0, 2, 2, 0)
    send_token(0, 2, 2, 1)
    send_token(0, 4, 4)
    send_token(0, 1, 1)
    g_copies = {}
    s_copies = {}
    for r in range(1, PLANE):
        g_copies[r] = remote(g_cols(r), G.at[tok_rows(0)], g_send.at[r], g_recv.at[r], peer(r))
        s_copies[r] = remote(seg, SG.at[tok_slot(0)], s_send.at[r], s_recv.at[r], peer(r))

    def half_rows(plane, half):
        py = y if half == 0 else 1 - y
        return pl.ds(pl.multiple_of((plane * 4 + py * 2) * rows, 2 * rows), 2 * rows)

    def up_copy(t, half):
        at = W.at[half_rows(z - t, half)]
        return remote(at, at, up_send.at[t, half], up_recv.at[t, half], above(z + 1))

    def down_copy(t, half):
        at = W.at[half_rows(z + t, half)]
        return remote(at, at, down_send.at[t, half], down_recv.at[t, half], above(z - 1))

    def up_arrival(t, half):
        at = W.at[half_rows(z - 1 - t, half)]
        return remote(at, at, up_send.at[t, half], up_recv.at[t, half], above(z - 1))

    def down_arrival(t, half):
        at = W.at[half_rows(z + 1 + t, half)]
        return remote(at, at, down_send.at[t, half], down_recv.at[t, half], above(z + 1))

    def has_up(t):
        return (z < chain - 1) & (z - t >= 0)

    def has_down(t):
        return (z > 0) & (z + t <= chain - 1)

    def send_chain(t, half):
        @pl.when(has_up(t))
        def _():
            up_copy(t, half).start()

        @pl.when(has_down(t))
        def _():
            down_copy(t, half).start()

    def recv_chain(t, half):
        @pl.when(z - 1 - t >= 0)
        def _():
            up_arrival(t, half).wait_recv()

        @pl.when(z + 1 + t <= chain - 1)
        def _():
            down_arrival(t, half).wait_recv()

    def wait_token(r, part=None):
        at = N.at[tok_piece(r, part)]
        i = part or 0
        remote(at, at, t_send.at[r, i], t_recv.at[r, i], peer(1)).wait_recv()

    def wait_weight(r):
        at = w_rows(r)
        for i, (lo, width) in enumerate(((0, qcols), (qcols, kcols), (qcols + kcols, kcols))):
            ref = W.at[at, pl.ds(lo, width)]
            remote(ref, ref, w_send.at[r, i], w_recv.at[r, i], peer(r)).wait_recv()

    part_rows = 4 * tok

    def part_at(part, i, height):
        py = y if part == 0 else 1 - y
        return pl.ds(pl.multiple_of(py * part_rows + i * height, height), height)

    def prepare(part):
        height = tok // 2

        @pl.loop(0, part_rows // height)
        def _(i):
            at = part_at(part, i, height)
            flt = N[at, :].astype(F32)
            meansq = jnp.sum(flt * flt, axis=-1, keepdims=True) / feats
            M[at, :] = (flt * lax.rsqrt(meansq + EPS) * gain[...].astype(F32)).astype(BF16)

        @pl.loop(0, part_rows // seq)
        def _(i):
            at = part_at(part, i, seq)
            block = M[at, :]
            LQ[at, :] = dot(block, qd[...], ((1,), (1,))).astype(BF16)
            LV[at, :] = dot(block, vd[...], ((1,), (1,))).astype(BF16)

    def add_piece(plane, half, part, first=False):
        chosen = half_rows(plane, half)

        @pl.loop(0, part_rows // seq)
        def _(i):
            at = part_at(part, i, seq)
            value = dot(M[at, chosen], W[chosen, :])
            acc[at, :] = value if first else acc[at, :] + value

    def add_step(t, half, part):
        @pl.when(z - 1 - t >= 0)
        def _():
            add_piece(z - 1 - t, half, part)

        @pl.when(z + 1 + t <= chain - 1)
        def _():
            add_piece(z + 1 + t, half, part)

    for i in range(3):
        local[i].wait()
    wait_weight(1)
    send_chain(0, 0)
    wait_weight(2)
    wait_weight(3)
    send_chain(0, 1)
    for r in range(1, PLANE):
        s_copies[r].start()
    recv_chain(0, 0)
    send_chain(1, 0)
    wait_token(4)
    send_token(4, 5, 1)
    wait_token(2, 0)
    send_token(2, 6, 4, 0)
    recv_chain(0, 1)
    send_chain(1, 1)
    local[3].wait()
    wait_token(1)
    wait_token(5)
    prepare(0)
    wait_token(2, 1)
    send_token(2, 6, 4, 1)
    send_token(2, 3, 1)
    for r in range(1, PLANE):
        g_copies[r].start()
    add_piece(z, 0, 0, True)
    add_piece(z, 1, 0)
    for half in range(2):
        add_step(0, half, 0)
    for t in range(1, chain - 2):
        for half in range(2):
            recv_chain(t, half)
            send_chain(t + 1, half)
            add_step(t, half, 0)
    wait_token(6, 0)
    wait_token(6, 1)
    send_token(6, 7, 1)
    wait_token(3)
    wait_token(7)
    prepare(1)
    add_piece(z, 0, 1, True)
    add_piece(z, 1, 1)
    for t in range(chain - 2):
        for half in range(2):
            add_step(t, half, 1)
    for half in range(2):
        recv_chain(chain - 2, half)
        for part in range(2):
            add_step(chain - 2, half, part)

    tiles = PLANE * tok // seq
    h = head_of(0)
    qu_own = qu[:, pl.ds(pl.multiple_of(h * qcols, qcols), qcols)]
    vu_own = vu[:, pl.ds(pl.multiple_of(h * kcols, kcols), kcols)]
    local[4].wait()
    local[5].wait()
    for r in range(1, PLANE):
        at = G.at[tok_rows(r)]
        remote(at, at, g_send.at[r], g_recv.at[r], peer(r)).wait_recv()
        at = SG.at[tok_slot(r)]
        remote(at, at, s_send.at[r], s_recv.at[r], peer(r)).wait_recv()

    pos_i = lax.broadcasted_iota(jnp.int32, (seq, seq), 0)
    pos_j = lax.broadcasted_iota(jnp.int32, (seq, seq), 1)
    band = (pos_j <= pos_i) & (pos_j > pos_i - 2 * tok)

    @pl.loop(0, tiles)
    def _(i):
        at = pl.ds(pl.multiple_of(i * seq, seq), seq)
        q_all = (acc[at, 0:qcols] + ADAPTER_NAME * dot(LQ[at, :], qu_own)).astype(BF16)
        k = acc[at, qcols:qcols + kcols].astype(BF16)
        v = (acc[at, qcols + kcols:] + ADAPTER_NAME * dot(LV[at, :], vu_own)).astype(BF16)
        g_all = G[at, :]
        traces = [SG[2 * i].astype(F32), SG[2 * i + 1].astype(F32)]
        along = jnp.concatenate(traces, axis=1)
        turned = [jnp.broadcast_to(own, (tok, tok)).T for own in traces]
        across = jnp.concatenate([jnp.concatenate([own, own], axis=1) for own in turned], axis=0)
        mask = band & (across == along)
        dv = jnp.zeros((seq, kcols), F32)
        for n in range(qcols // kcols):
            q = q_all[:, n * kcols:(n + 1) * kcols]
            g = g_all[:, n * kcols:(n + 1) * kcols]
            s = dot(q, k, ((1,), (1,))) * QSCALE
            t = jnp.tanh(s / CAP)
            expo = jnp.where(mask, jnp.exp(CAP * t), 0.0)
            weights = expo / jnp.sum(expo, axis=-1, keepdims=True)
            weights16 = weights.astype(BF16)
            attended = dot(weights16, v)
            dweight = dot(g, v, ((1,), (1,)))
            delta = jnp.sum(g.astype(F32) * attended, axis=-1, keepdims=True)
            dscore = (weights * (dweight - delta) * (1.0 - t * t) * QSCALE).astype(BF16)
            DQ[at, n * kcols:(n + 1) * kcols] = dot(dscore, k).astype(BF16)
            dv = dv + dot(weights16, g, ((0,), (0,)))
        DV[at, :] = dv.astype(BF16)

    pull_q = dot(qu_own, DQ[...], ((1,), (1,))).astype(BF16)
    pull_v = dot(vu_own, DV[...], ((1,), (1,))).astype(BF16)
    pull = jnp.concatenate([pull_q, pull_v], axis=0)
    ranks = pull.shape[0]
    half_rank = ranks // 2
    r1_copies = []
    for r in (7, 6, 5, 4, 3, 2, 1, 0):
        columns = pl.ds(pl.multiple_of(head_of(r) * piece, piece), piece)
        A[r] = dot(pull, M[:, columns]).astype(BF16)
        if r > 0:
            copy = remote(A.at[r], RA.at[r], r1_send.at[r], r1_recv.at[r], peer(r))
            copy.start()
            r1_copies.append(copy)
    own_sum = RS.at[z]
    own_sum[ranks:, 0:qcols] = dot(LQ[...], DQ[...], ((0,), (0,))).astype(BF16)
    own_sum[ranks:, qcols:qcols + kcols] = dot(LV[...], DV[...], ((0,), (0,))).astype(BF16)
    for copy in r1_copies:
        copy.wait_recv()
    total = A[0].astype(F32)
    for r in range(1, PLANE):
        total = total + RA[r].astype(F32)
    own_sum[0:ranks, :] = total.astype(BF16)
    r2_copies = []
    for d in range(1, chain):
        copy = remote(own_sum, own_sum, r2_send.at[d], r2_recv.at[d], above((z + d) % chain))
        copy.start()
        r2_copies.append(copy)
    for d in range(1, chain):
        at = RS.at[(z - d + chain) % chain]
        remote(at, at, r2_send.at[d], r2_recv.at[d], above((z + d) % chain)).wait_recv()
    total = RS[0].astype(F32)
    for d in range(1, chain):
        total = total + RS[d].astype(F32)
    total = (total * coefficient).astype(BF16)
    T[...] = total
    r3_copies = []
    for r in (7, 6, 5, 4, 3, 2, 1):
        copy = remote(T, OUT.at[h], r3_send.at[r], r3_recv.at[r], peer(r))
        copy.start()
        r3_copies.append(copy)
    OUT[h] = total
    for r in range(1, PLANE):
        at = OUT.at[head_of(r)]
        remote(at, at, r3_send.at[r], r3_recv.at[r], peer(r)).wait_recv()

    for r in (1, 2, 3):
        for copy in w_copies[r]:
            copy.wait_send()
    for copy in t_copies:
        copy.wait_send()
    for r in range(1, PLANE):
        g_copies[r].wait_send()
        s_copies[r].wait_send()
    for t in range(chain - 1):
        for half in range(2):
            @pl.when(has_up(t))
            def _():
                up_copy(t, half).wait_send()

            @pl.when(has_down(t))
            def _():
                down_copy(t, half).wait_send()
    for copy in r1_copies + r2_copies + r3_copies:
        copy.wait_send()


def unpack_kernel(gathered, out_aq, out_bq, out_av, out_bv):
    ranks, feats = out_aq.shape
    piece = feats // PLANE
    qcols = out_bq.shape[1] // PLANE
    kcols = out_bv.shape[1] // PLANE
    for h in range(PLANE):
        value = gathered[h].astype(F32)
        out_aq[:, h * piece:(h + 1) * piece] = value[0:ranks]
        out_av[:, h * piece:(h + 1) * piece] = value[ranks:2 * ranks]
        out_bq[:, h * qcols:(h + 1) * qcols] = value[2 * ranks:, 0:qcols]
        out_bv[:, h * kcols:(h + 1) * kcols] = value[2 * ranks:, qcols:qcols + kcols]


def on_plane(
    tokens,
    trace_index,
    input_norm_scale,
    query_weight,
    key_weight,
    value_weight,
    query_down_weight,
    query_up_weight,
    value_down_weight,
    value_up_weight,
    output_gradient,
):
    tok = tokens.shape[1]
    feats = tokens.shape[2]
    fsdp = lax.axis_size("fsdp")
    chain = fsdp // 4
    ranks = query_down_weight.shape[1]
    qcols = query_weight.shape[1] // PLANE
    kcols = key_weight.shape[1] // PLANE
    columns = qcols + 2 * kcols
    piece = feats // PLANE
    many = PLANE * tok
    token_total = lax.axis_size("ctx") * fsdp * tok
    coefficient = ADAPTER_NAME / math.sqrt(token_total)
    hbm = pl.BlockSpec(memory_space=pl.ANY)
    vmem = pl.BlockSpec(memory_space=pltpu.VMEM)
    dma = pltpu.SemaphoreType.DMA
    steps = max(chain - 1, 1)
    gathered = pl.pallas_call(
        functools.partial(plane_kernel, chain, coefficient),
        out_shape=jax.ShapeDtypeStruct((PLANE, 3 * ranks, piece), BF16),
        in_specs=[hbm, hbm, vmem, hbm, hbm, hbm, vmem, vmem, vmem, vmem, hbm],
        out_specs=vmem,
        scratch_shapes=[
            pltpu.VMEM((many, feats), BF16),
            pltpu.VMEM((many, feats), BF16),
            pltpu.VMEM((feats, columns), BF16),
            pltpu.VMEM((many, qcols), BF16),
            pltpu.VMEM((PLANE, 1, tok), jnp.int32),
            pltpu.VMEM((many, columns), F32),
            pltpu.VMEM((many, qcols), BF16),
            pltpu.VMEM((many, kcols), BF16),
            pltpu.VMEM((many, ranks), BF16),
            pltpu.VMEM((many, ranks), BF16),
            pltpu.VMEM((PLANE, 2 * ranks, piece), BF16),
            pltpu.VMEM((PLANE, 2 * ranks, piece), BF16),
            pltpu.VMEM((chain, 3 * ranks, piece), BF16),
            pltpu.VMEM((3 * ranks, piece), BF16),
            dma((6,)),
            dma((4, 3)), dma((4, 3)),
            dma((8, 2)), dma((8, 2)), dma((8,)), dma((8,)), dma((8,)), dma((8,)),
            dma((steps, 2)), dma((steps, 2)), dma((steps, 2)), dma((steps, 2)),
            dma((8,)), dma((8,)), dma((max(chain, 2),)), dma((max(chain, 2),)), dma((8,)), dma((8,)),
        ],
        compiler_params=pltpu.CompilerParams(
            collective_id=0, has_side_effects=True, vmem_limit_bytes=56 * 1024 * 1024
        ),
    )(
        tokens.reshape(tok, feats), trace_index, input_norm_scale.reshape(1, feats),
        query_weight, key_weight, value_weight,
        query_down_weight.T, query_up_weight, value_down_weight.T, value_up_weight,
        output_gradient.reshape(tok, output_gradient.shape[2]),
    )
    aq, bq, av, bv = pl.pallas_call(
        unpack_kernel,
        out_shape=(
            jax.ShapeDtypeStruct((ranks, feats), F32),
            jax.ShapeDtypeStruct((ranks, query_weight.shape[1]), F32),
            jax.ShapeDtypeStruct((ranks, feats), F32),
            jax.ShapeDtypeStruct((ranks, value_weight.shape[1]), F32),
        ),
        in_specs=[vmem],
        out_specs=(vmem, vmem, vmem, vmem),
    )(gathered)
    return (aq.T, bq, av.T, bv)


def solution(mesh):
    shape = mesh.shape
    planes = shape["groups"] == 1 and shape["ctx"] == 2 and shape["fsdp"] % 4 == 0 and shape["fsdp"] > 8
    return jax.shard_map(
        on_plane if planes else on_device,
        mesh=mesh,
        in_specs=(
            P(("groups", "fsdp"), "ctx", None),
            P(("groups", "fsdp"), "ctx"),
            P(),
            P("fsdp", None),
            P("fsdp", None),
            P("fsdp", None),
            P(),
            P(),
            P(),
            P(),
            P(("groups", "fsdp"), "ctx", None),
        ),
        out_specs=(P("groups", None), P("groups", None), P("groups", None), P("groups", None)),
        check_vma=False,
    )
```

```python
import functools
import math

import jax
import jax.numpy as jnp
from jax import lax
from jax.experimental import pallas as pl
from jax.experimental.pallas import tpu as pltpu
from jax.sharding import PartitionSpec as P

HEAD_SIZE = 128


CAP = 50.0
QSCALE = 1.0 / 12.0
ADAPTER_NAME = 0.5
EPS = 1e-06


def shifted(value, axis, by):
    devices = lax.axis_size(axis)
    pairs = [(i, i + by) for i in range(devices) if 0 <= i + by < devices]
    return lax.ppermute(value, axis, pairs)


def normed_rows(values, gain):
    flt = values.astype(jnp.float32)
    meansq = jnp.mean(flt * flt, axis=-1, keepdims=True)
    return (flt * lax.rsqrt(meansq + EPS) * gain.astype(jnp.float32)).astype(jnp.bfloat16)


def add_rows(left, piece):
    return jnp.dot(left, piece, preferred_element_type=jnp.float32)


def attend_head(operands, mask):
    q_head, k_head, v_head, g_head = operands
    s = jnp.einsum("igd,jd->gij", q_head, k_head, preferred_element_type=jnp.float32) * QSCALE
    t = jnp.tanh(s / CAP)
    capped = CAP * t
    expo = jnp.where(mask[None], jnp.exp(capped), jnp.float32(0.0))
    weights = expo / jnp.sum(expo, axis=-1, keepdims=True)
    weights16 = weights.astype(jnp.bfloat16)
    attended = jnp.einsum("gij,jd->igd", weights16, v_head, preferred_element_type=jnp.float32)
    dweight = jnp.einsum("igd,jd->gij", g_head, v_head, preferred_element_type=jnp.float32)
    delta = jnp.sum(g_head.astype(jnp.float32) * attended, axis=-1).T
    dscore = (weights * (dweight - delta[..., None]) * (1.0 - t * t) * QSCALE).astype(jnp.bfloat16)
    query_gradient = jnp.einsum(
        "gij,jd->igd", dscore, k_head, preferred_element_type=jnp.float32
    ).astype(jnp.bfloat16)
    value_gradient = jnp.einsum(
        "gij,igd->jd", weights16, g_head, preferred_element_type=jnp.float32
    )
    return (query_gradient, value_gradient)


def partial_attend(mask):

    def run_head(operands):
        return attend_head(operands, mask)

    return run_head


def on_device(
    tokens,
    trace_index,
    input_norm_scale,
    query_weight,
    key_weight,
    value_weight,
    query_down_weight,
    query_up_weight,
    value_down_weight,
    value_up_weight,
    output_gradient,
):
    window_width = tokens.shape[1]
    feats = tokens.shape[2]
    heads_kv = key_weight.shape[1] // HEAD_SIZE
    heads_q = query_weight.shape[1] // HEAD_SIZE
    head_group = heads_q // heads_kv
    normalized_input = normed_rows(tokens.reshape(window_width, feats), input_norm_scale)
    seg_own = trace_index.reshape(window_width).astype(jnp.bfloat16)
    seg_parts = []

    def add_keyval(piece):
        return add_rows(normalized_input, piece)

    query_frozen = add_rows(
        normalized_input, lax.all_gather(query_weight, "fsdp", axis=0, tiled=True)
    )
    k_base = add_keyval(lax.all_gather(key_weight, "fsdp", axis=0, tiled=True))
    value_frozen = add_keyval(lax.all_gather(value_weight, "fsdp", axis=0, tiled=True))
    query_reduced = jnp.dot(
        normalized_input, query_down_weight, preferred_element_type=jnp.float32
    ).astype(jnp.bfloat16)
    reduced_rows = jnp.dot(
        normalized_input, value_down_weight, preferred_element_type=jnp.float32
    ).astype(jnp.bfloat16)
    query_matrix = (
        query_frozen
        + ADAPTER_NAME * jnp.dot(query_reduced, query_up_weight, preferred_element_type=jnp.float32)
    ).astype(jnp.bfloat16)
    key_rows = k_base.astype(jnp.bfloat16)
    value_rows = (
        value_frozen
        + ADAPTER_NAME * jnp.dot(reduced_rows, value_up_weight, preferred_element_type=jnp.float32)
    ).astype(jnp.bfloat16)
    key_parts = []
    value_parts = []
    for distance in (2, 1):
        key_prev, value_prev, seg_prev = shifted((key_rows, value_rows, seg_own), "ctx", distance)
        key_parts.append(key_prev)
        value_parts.append(value_prev)
        seg_parts.append(seg_prev)
    keys_all = jnp.concatenate(key_parts + [key_rows], 0)
    values_all = jnp.concatenate(value_parts + [value_rows], 0)
    seg_keys = jnp.concatenate(seg_parts + [seg_own], 0)
    pos_q = jnp.arange(window_width, dtype=jnp.int32)[:, None]
    pos_k = jnp.arange(3 * window_width, dtype=jnp.int32)[None, :]
    position = lax.axis_index("ctx")
    mask = (
        (pos_k > pos_q)
        & (pos_k <= pos_q + 2 * window_width)
        & (seg_keys[None, :] == seg_own[:, None])
    )
    mask = mask & (
        (pos_k >= 2 * window_width) | (pos_k >= window_width) & (position >= 1) | (position >= 2)
    )
    q_heads = jnp.moveaxis(
        query_matrix.reshape(window_width, heads_kv, head_group, HEAD_SIZE), 1, 0
    )
    g_heads = jnp.moveaxis(
        output_gradient.reshape(window_width, heads_kv, head_group, HEAD_SIZE), 1, 0
    )
    k_heads = jnp.moveaxis(keys_all.reshape(3 * window_width, heads_kv, HEAD_SIZE), 1, 0)
    v_heads = jnp.moveaxis(values_all.reshape(3 * window_width, heads_kv, HEAD_SIZE), 1, 0)
    dquery_heads, dvalue_heads = lax.map(partial_attend(mask), (q_heads, k_heads, v_heads, g_heads))
    query_gradient = jnp.moveaxis(dquery_heads, 0, 1).reshape(window_width, heads_q * HEAD_SIZE)
    dvalue_triple = jnp.moveaxis(dvalue_heads, 0, 1).reshape(3 * window_width, heads_kv * HEAD_SIZE)
    value_gradient = dvalue_triple[2 * window_width :]
    for distance in (1, 2):
        begin = (2 - distance) * window_width
        value_gradient = value_gradient + shifted(
            dvalue_triple[begin : begin + window_width], "ctx", -distance
        )
    query_backward = jnp.dot(
        query_gradient, query_up_weight.T, preferred_element_type=jnp.float32
    ).astype(jnp.bfloat16)
    value_backward = jnp.dot(
        value_gradient, value_up_weight.astype(jnp.float32).T, precision=lax.Precision.HIGHEST
    )
    part_aq = jnp.dot(normalized_input.T, query_backward, preferred_element_type=jnp.float32)
    part_bq = jnp.dot(query_reduced.T, query_gradient, preferred_element_type=jnp.float32)
    part_av = jnp.dot(
        normalized_input.astype(jnp.float32).T, value_backward, precision=lax.Precision.HIGHEST
    )
    part_bv = jnp.dot(
        reduced_rows.astype(jnp.float32).T, value_gradient, precision=lax.Precision.HIGHEST
    )
    sum_aq, sum_bq, sum_av, sum_bv = lax.psum((part_aq, part_bq, part_av, part_bv), ("ctx", "fsdp"))
    token_total = lax.axis_size("ctx") * lax.axis_size("fsdp") * window_width
    coefficient = ADAPTER_NAME / math.sqrt(token_total)
    return (sum_aq * coefficient, sum_bq * coefficient, sum_av * coefficient, sum_bv * coefficient)


F32 = jnp.float32
BF16 = jnp.bfloat16
PLANE = 8


def dot(a, b, dims=((1,), (0,))):
    return lax.dot_general(a, b, (dims, ((), ())), preferred_element_type=F32)


def plane_kernel(
    chain, coefficient,
    raw, seg, gain, wq, wk, wv, qd, qu, vd, vu, grad,
    OUT,
    N, M, W, G, SG, acc, DQ, DV, LQ, LV, A, RA, RS, T,
    local_sem, w_send, w_recv, t_send, t_recv, g_send, g_recv, s_send, s_recv,
    up_send, up_recv, down_send, down_recv,
    r1_send, r1_recv, r2_send, r2_recv, r3_send, r3_recv,
):
    x = lax.axis_index("ctx")
    f = lax.axis_index("fsdp")
    z = f // 4
    y = (f // 2) % 2
    c = f % 2
    tok, feats = raw.shape
    rows = wq.shape[0]
    qcols = wq.shape[1] // PLANE
    kcols = wk.shape[1] // PLANE
    piece = feats // PLANE
    plane_rows = 4 * rows
    seq = 2 * tok

    def coords(r):
        px = 1 - x if r & 4 else x
        py = 1 - y if r & 2 else y
        pc = 1 - c if r & 1 else c
        return px, py, pc

    def head_of(r):
        px, py, pc = coords(r)
        return (px * 2 + py) * 2 + pc

    def peer(r):
        px, py, pc = coords(r)
        return {"ctx": px, "fsdp": (z * 2 + py) * 2 + pc}

    def above(pz):
        return {"ctx": x, "fsdp": (pz * 2 + y) * 2 + c}

    def tok_rows(r):
        px, py, pc = coords(r)
        return pl.ds(pl.multiple_of(((py * 2 + pc) * 2 + px) * tok, tok), tok)

    def tok_slot(r):
        px, py, pc = coords(r)
        return (py * 2 + pc) * 2 + px

    def tok_piece(r, part):
        px, py, pc = coords(r)
        if part is None:
            return tok_rows(r)
        begin = ((py * 2 + pc) * 2 + px) * tok + part * (tok // 2)
        return pl.ds(pl.multiple_of(begin, tok // 2), tok // 2)

    def remote(src, dst, send, recv, device):
        return pltpu.make_async_remote_copy(
            src_ref=src, dst_ref=dst, send_sem=send, recv_sem=recv,
            device_id=device, device_id_type=pl.DeviceIdType.MESH,
        )

    barrier = pltpu.get_barrier_semaphore()
    for r in range(1, PLANE):
        pl.semaphore_signal(barrier, inc=1, device_id=peer(r), device_id_type=pl.DeviceIdType.MESH)
    for d in range(1, chain):
        pl.semaphore_signal(
            barrier, inc=1, device_id=above((z + d) % chain), device_id_type=pl.DeviceIdType.MESH
        )

    def w_rows(r):
        px, py, pc = coords(r)
        return pl.ds(pl.multiple_of(((z * 2 + py) * 2 + pc) * rows, rows), rows)

    def w_parts(r):
        h = head_of(r)
        own = w_rows(0)
        return (
            (wq.at[:, pl.ds(pl.multiple_of(h * qcols, qcols), qcols)], W.at[own, pl.ds(0, qcols)]),
            (wk.at[:, pl.ds(pl.multiple_of(h * kcols, kcols), kcols)], W.at[own, pl.ds(qcols, kcols)]),
            (wv.at[:, pl.ds(pl.multiple_of(h * kcols, kcols), kcols)], W.at[own, pl.ds(qcols + kcols, kcols)]),
        )

    def g_cols(r):
        h = head_of(r)
        return grad.at[:, pl.ds(pl.multiple_of(h * qcols, qcols), qcols)]

    local = [pltpu.make_async_copy(a, b, local_sem.at[i]) for i, (a, b) in enumerate(w_parts(0))]
    local.append(pltpu.make_async_copy(raw, N.at[tok_rows(0)], local_sem.at[3]))
    local.append(pltpu.make_async_copy(g_cols(0), G.at[tok_rows(0)], local_sem.at[4]))
    local.append(pltpu.make_async_copy(seg, SG.at[tok_slot(0)], local_sem.at[5]))
    for copy in local:
        copy.start()
    pl.semaphore_wait(barrier, PLANE - 1 + chain - 1)

    w_copies = {}
    for r in (1, 2, 3):
        w_copies[r] = [
            remote(a, b, w_send.at[r, i], w_recv.at[r, i], peer(r)) for i, (a, b) in enumerate(w_parts(r))
        ]
        for copy in w_copies[r]:
            copy.start()
    t_copies = []

    def send_token(r_mine, r_there, hop, part=None):
        at = N.at[tok_piece(r_mine, part)]
        source = at
        if r_mine == 0:
            source = raw if part is None else raw.at[pl.ds(part * (tok // 2), tok // 2)]
        i = part or 0
        copy = remote(source, at, t_send.at[r_there, i], t_recv.at[r_there, i], peer(hop))
        copy.start()
        t_copies.append(copy)

    send_token(0, 2, 2, 0)
    send_token(0, 2, 2, 1)
    send_token(0, 4, 4)
    send_token(0, 1, 1)
    g_copies = {}
    s_copies = {}
    for r in range(1, PLANE):
        g_copies[r] = remote(g_cols(r), G.at[tok_rows(0)], g_send.at[r], g_recv.at[r], peer(r))
        s_copies[r] = remote(seg, SG.at[tok_slot(0)], s_send.at[r], s_recv.at[r], peer(r))

    def half_rows(plane, half):
        py = y if half == 0 else 1 - y
        return pl.ds(pl.multiple_of((plane * 4 + py * 2) * rows, 2 * rows), 2 * rows)

    def up_copy(t, half):
        at = W.at[half_rows(z - t, half)]
        return remote(at, at, up_send.at[t, half], up_recv.at[t, half], above(z + 1))

    def down_copy(t, half):
        at = W.at[half_rows(z + t, half)]
        return remote(at, at, down_send.at[t, half], down_recv.at[t, half], above(z - 1))

    def up_arrival(t, half):
        at = W.at[half_rows(z - 1 - t, half)]
        return remote(at, at, up_send.at[t, half], up_recv.at[t, half], above(z - 1))

    def down_arrival(t, half):
        at = W.at[half_rows(z + 1 + t, half)]
        return remote(at, at, down_send.at[t, half], down_recv.at[t, half], above(z + 1))

    def has_up(t):
        return (z < chain - 1) & (z - t >= 0)

    def has_down(t):
        return (z > 0) & (z + t <= chain - 1)

    def send_chain(t, half):
        @pl.when(has_up(t))
        def _():
            up_copy(t, half).start()

        @pl.when(has_down(t))
        def _():
            down_copy(t, half).start()

    def recv_chain(t, half):
        @pl.when(z - 1 - t >= 0)
        def _():
            up_arrival(t, half).wait_recv()

        @pl.when(z + 1 + t <= chain - 1)
        def _():
            down_arrival(t, half).wait_recv()

    def wait_token(r, part=None):
        at = N.at[tok_piece(r, part)]
        i = part or 0
        remote(at, at, t_send.at[r, i], t_recv.at[r, i], peer(1)).wait_recv()

    def wait_weight(r):
        at = w_rows(r)
        for i, (lo, width) in enumerate(((0, qcols), (qcols, kcols), (qcols + kcols, kcols))):
            ref = W.at[at, pl.ds(lo, width)]
            remote(ref, ref, w_send.at[r, i], w_recv.at[r, i], peer(r)).wait_recv()

    part_rows = 4 * tok

    def part_at(part, i, height):
        py = y if part == 0 else 1 - y
        return pl.ds(pl.multiple_of(py * part_rows + i * height, height), height)

    def prepare(r):
        height = tok // 2

        @pl.loop(0, 2)
        def _(i):
            px, py, pc = coords(r)
            begin = ((py * 2 + pc) * 2 + px) * tok + i * height
            at = pl.ds(pl.multiple_of(begin, height), height)
            flt = N[at, :].astype(F32)
            meansq = jnp.sum(flt * flt, axis=-1, keepdims=True) / feats
            M[at, :] = (flt * lax.rsqrt(meansq + EPS) * gain[...].astype(F32).reshape(1, feats)).astype(BF16)

        at = tok_rows(r)
        block = M[at, :]
        LQ[at, :] = dot(block, qd[...], ((1,), (1,))).astype(BF16)
        LV[at, :] = dot(block, vd[...], ((1,), (1,))).astype(BF16)

    def add_piece(plane, half, part, first=False):
        chosen = half_rows(plane, half)

        @pl.loop(0, part_rows // seq)
        def _(i):
            at = part_at(part, i, seq)
            value = dot(M[at, chosen], W[chosen, :])
            acc[at, :] = value if first else acc[at, :] + value

    def add_step(t, half, part):
        @pl.when(z - 1 - t >= 0)
        def _():
            add_piece(z - 1 - t, half, part)

        @pl.when(z + 1 + t <= chain - 1)
        def _():
            add_piece(z + 1 + t, half, part)

    for i in range(3):
        local[i].wait()
    wait_weight(1)
    send_chain(0, 0)
    wait_weight(2)
    wait_weight(3)
    send_chain(0, 1)
    for r in range(1, PLANE):
        s_copies[r].start()
    recv_chain(0, 0)
    send_chain(1, 0)
    local[3].wait()
    prepare(0)
    wait_token(1)
    prepare(1)
    wait_token(4)
    send_token(4, 5, 1)
    wait_token(2, 0)
    send_token(2, 6, 4, 0)
    recv_chain(0, 1)
    send_chain(1, 1)
    prepare(4)
    wait_token(5)
    prepare(5)
    wait_token(2, 1)
    send_token(2, 6, 4, 1)
    send_token(2, 3, 1)
    for r in range(1, PLANE):
        g_copies[r].start()
    prepare(2)
    add_piece(z, 0, 0, True)
    add_piece(z, 1, 0)
    for half in range(2):
        add_step(0, half, 0)
    wait_token(3)
    prepare(3)
    for t in range(1, chain - 2):
        for half in range(2):
            recv_chain(t, half)
            send_chain(t + 1, half)
            add_step(t, half, 0)
    wait_token(6, 0)
    wait_token(6, 1)
    send_token(6, 7, 1)
    prepare(6)
    wait_token(7)
    prepare(7)
    add_piece(z, 0, 1, True)
    add_piece(z, 1, 1)
    for t in range(chain - 2):
        for half in range(2):
            add_step(t, half, 1)
    for half in range(2):
        recv_chain(chain - 2, half)
        for part in range(2):
            add_step(chain - 2, half, part)

    tiles = PLANE * tok // seq
    h = head_of(0)
    qu_own = qu[:, pl.ds(pl.multiple_of(h * qcols, qcols), qcols)]
    vu_own = vu[:, pl.ds(pl.multiple_of(h * kcols, kcols), kcols)]
    local[4].wait()
    local[5].wait()
    for r in range(1, PLANE):
        at = G.at[tok_rows(r)]
        remote(at, at, g_send.at[r], g_recv.at[r], peer(r)).wait_recv()
        at = SG.at[tok_slot(r)]
        remote(at, at, s_send.at[r], s_recv.at[r], peer(r)).wait_recv()

    pos_i = lax.broadcasted_iota(jnp.int32, (seq, seq), 0)
    pos_j = lax.broadcasted_iota(jnp.int32, (seq, seq), 1)
    band = (pos_j <= pos_i) & (pos_j > pos_i - 2 * tok)

    @pl.loop(0, tiles, unroll=2)
    def _(i):
        at = pl.ds(pl.multiple_of(i * seq, seq), seq)
        q_all = (acc[at, 0:qcols] + ADAPTER_NAME * dot(LQ[at, :], qu_own)).astype(BF16)
        k = acc[at, qcols:qcols + kcols].astype(BF16)
        v = (acc[at, qcols + kcols:] + ADAPTER_NAME * dot(LV[at, :], vu_own)).astype(BF16)
        g_all = G[at, :]
        traces = [SG[2 * i].astype(F32), SG[2 * i + 1].astype(F32)]
        along = jnp.concatenate(traces, axis=1)
        turned = [jnp.broadcast_to(own, (tok, tok)).T for own in traces]
        across = jnp.concatenate([jnp.concatenate([own, own], axis=1) for own in turned], axis=0)
        mask = band & (across == along)
        dv = jnp.zeros((seq, kcols), F32)
        for n in range(qcols // kcols):
            q = q_all[:, n * kcols:(n + 1) * kcols]
            g = g_all[:, n * kcols:(n + 1) * kcols]
            t = jnp.tanh(dot(q, k, ((1,), (1,))) * (QSCALE / CAP))
            expo = jnp.where(mask, jnp.exp(CAP * t), 0.0)
            weights = expo * (1.0 / jnp.sum(expo, axis=-1, keepdims=True))
            weights16 = weights.astype(BF16)
            attended = dot(weights16, v)
            dweight = dot(g, v, ((1,), (1,)))
            delta = jnp.sum(g.astype(F32) * attended, axis=-1, keepdims=True)
            dscore = (weights * (dweight - delta) * (1.0 - t * t)).astype(BF16)
            DQ[at, n * kcols:(n + 1) * kcols] = (dot(dscore, k) * QSCALE).astype(BF16)
            dv = dv + dot(weights16, g, ((0,), (0,)))
        DV[at, :] = dv.astype(BF16)

    pull_q = dot(qu_own, DQ[...], ((1,), (1,))).astype(BF16)
    pull_v = dot(vu_own, DV[...], ((1,), (1,))).astype(BF16)
    pull = jnp.concatenate([pull_q, pull_v], axis=0)
    ranks = pull.shape[0]
    half_rank = ranks // 2
    r1_copies = []
    for r in (7, 6, 5, 4, 3, 2, 1, 0):
        columns = pl.ds(pl.multiple_of(head_of(r) * piece, piece), piece)
        A[r] = dot(pull, M[:, columns]).astype(BF16)
        if r > 0:
            copy = remote(A.at[r], RA.at[r], r1_send.at[r], r1_recv.at[r], peer(r))
            copy.start()
            r1_copies.append(copy)
    own_sum = RS.at[z]
    own_sum[ranks:, 0:qcols] = dot(LQ[...], DQ[...], ((0,), (0,))).astype(BF16)
    own_sum[ranks:, qcols:qcols + kcols] = dot(LV[...], DV[...], ((0,), (0,))).astype(BF16)
    for copy in r1_copies:
        copy.wait_recv()
    total = A[0].astype(F32)
    for r in range(1, PLANE):
        total = total + RA[r].astype(F32)
    own_sum[0:ranks, :] = total.astype(BF16)
    r2_copies = []
    for d in range(1, chain):
        copy = remote(own_sum, own_sum, r2_send.at[d], r2_recv.at[d], above((z + d) % chain))
        copy.start()
        r2_copies.append(copy)
    for d in range(1, chain):
        at = RS.at[(z - d + chain) % chain]
        remote(at, at, r2_send.at[d], r2_recv.at[d], above((z + d) % chain)).wait_recv()
    total = RS[0].astype(F32)
    for d in range(1, chain):
        total = total + RS[d].astype(F32)
    total = (total * coefficient).astype(BF16)
    T[...] = total
    r3_copies = []
    for r in (7, 6, 5, 4, 3, 2, 1):
        copy = remote(T, OUT.at[h], r3_send.at[r], r3_recv.at[r], peer(r))
        copy.start()
        r3_copies.append(copy)
    OUT[h] = total
    for r in range(1, PLANE):
        at = OUT.at[head_of(r)]
        remote(at, at, r3_send.at[r], r3_recv.at[r], peer(r)).wait_recv()

    for r in (1, 2, 3):
        for copy in w_copies[r]:
            copy.wait_send()
    for copy in t_copies:
        copy.wait_send()
    for r in range(1, PLANE):
        g_copies[r].wait_send()
        s_copies[r].wait_send()
    for t in range(chain - 1):
        for half in range(2):
            @pl.when(has_up(t))
            def _():
                up_copy(t, half).wait_send()

            @pl.when(has_down(t))
            def _():
                down_copy(t, half).wait_send()
    for copy in r1_copies + r2_copies + r3_copies:
        copy.wait_send()


def unpack_kernel(gathered, out_aq, out_bq, out_av, out_bv):
    ranks, feats = out_aq.shape
    piece = feats // PLANE
    qcols = out_bq.shape[1] // PLANE
    kcols = out_bv.shape[1] // PLANE
    for h in range(PLANE):
        value = gathered[h].astype(F32)
        out_aq[:, h * piece:(h + 1) * piece] = value[0:ranks]
        out_av[:, h * piece:(h + 1) * piece] = value[ranks:2 * ranks]
        out_bq[:, h * qcols:(h + 1) * qcols] = value[2 * ranks:, 0:qcols]
        out_bv[:, h * kcols:(h + 1) * kcols] = value[2 * ranks:, qcols:qcols + kcols]


def on_plane(
    tokens,
    trace_index,
    input_norm_scale,
    query_weight,
    key_weight,
    value_weight,
    query_down_weight,
    query_up_weight,
    value_down_weight,
    value_up_weight,
    output_gradient,
):
    tok = tokens.shape[1]
    feats = tokens.shape[2]
    fsdp = lax.axis_size("fsdp")
    chain = fsdp // 4
    ranks = query_down_weight.shape[1]
    qcols = query_weight.shape[1] // PLANE
    kcols = key_weight.shape[1] // PLANE
    columns = qcols + 2 * kcols
    piece = feats // PLANE
    many = PLANE * tok
    token_total = lax.axis_size("ctx") * fsdp * tok
    coefficient = ADAPTER_NAME / math.sqrt(token_total)
    hbm = pl.BlockSpec(memory_space=pl.ANY)
    vmem = pl.BlockSpec(memory_space=pltpu.VMEM)
    dma = pltpu.SemaphoreType.DMA
    steps = max(chain - 1, 1)
    gathered = pl.pallas_call(
        functools.partial(plane_kernel, chain, coefficient),
        out_shape=jax.ShapeDtypeStruct((PLANE, 3 * ranks, piece), BF16),
        in_specs=[hbm, hbm, vmem, hbm, hbm, hbm, vmem, vmem, vmem, vmem, hbm],
        out_specs=vmem,
        scratch_shapes=[
            pltpu.VMEM((many, feats), BF16),
            pltpu.VMEM((many, feats), BF16),
            pltpu.VMEM((feats, columns), BF16),
            pltpu.VMEM((many, qcols), BF16),
            pltpu.VMEM((PLANE, 1, tok), jnp.int32),
            pltpu.VMEM((many, columns), F32),
            pltpu.VMEM((many, qcols), BF16),
            pltpu.VMEM((many, kcols), BF16),
            pltpu.VMEM((many, ranks), BF16),
            pltpu.VMEM((many, ranks), BF16),
            pltpu.VMEM((PLANE, 2 * ranks, piece), BF16),
            pltpu.VMEM((PLANE, 2 * ranks, piece), BF16),
            pltpu.VMEM((chain, 3 * ranks, piece), BF16),
            pltpu.VMEM((3 * ranks, piece), BF16),
            dma((6,)),
            dma((4, 3)), dma((4, 3)),
            dma((8, 2)), dma((8, 2)), dma((8,)), dma((8,)), dma((8,)), dma((8,)),
            dma((steps, 2)), dma((steps, 2)), dma((steps, 2)), dma((steps, 2)),
            dma((8,)), dma((8,)), dma((max(chain, 2),)), dma((max(chain, 2),)), dma((8,)), dma((8,)),
        ],
        compiler_params=pltpu.CompilerParams(
            collective_id=0, has_side_effects=True, vmem_limit_bytes=56 * 1024 * 1024
        ),
    )(
        tokens.reshape(tok, feats), trace_index, input_norm_scale,
        query_weight, key_weight, value_weight,
        query_down_weight.T, query_up_weight, value_down_weight.T, value_up_weight,
        output_gradient.reshape(tok, output_gradient.shape[2]),
    )
    aq, bq, av, bv = pl.pallas_call(
        unpack_kernel,
        out_shape=(
            jax.ShapeDtypeStruct((ranks, feats), F32),
            jax.ShapeDtypeStruct((ranks, query_weight.shape[1]), F32),
            jax.ShapeDtypeStruct((ranks, feats), F32),
            jax.ShapeDtypeStruct((ranks, value_weight.shape[1]), F32),
        ),
        in_specs=[vmem],
        out_specs=(vmem, vmem, vmem, vmem),
    )(gathered)
    return (aq.T, bq, av.T, bv)


def solution(mesh):
    shape = mesh.shape
    planes = shape["groups"] == 1 and shape["ctx"] == 2 and shape["fsdp"] % 4 == 0 and shape["fsdp"] > 8
    return jax.shard_map(
        on_plane if planes else on_device,
        mesh=mesh,
        in_specs=(
            P(("groups", "fsdp"), "ctx", None),
            P(("groups", "fsdp"), "ctx"),
            P(),
            P("fsdp", None),
            P("fsdp", None),
            P("fsdp", None),
            P(),
            P(),
            P(),
            P(),
            P(("groups", "fsdp"), "ctx", None),
        ),
        out_specs=(P("groups", None), P("groups", None), P("groups", None), P("groups", None)),
        check_vma=False,
    )
```
